32 devices in a mesh: replica: 4 (over y, x), fsdp: 8 (over z, core).
Axes of the slice: x: 2, y: 2, z: 4, core: 2. Of those that a mesh axis runs over, the one named last changes fastest.
Arguments:
- partner: int32 [4], replicated, may hold values from 0 to 3, as said below
- tokens: bfloat16 [4, 128, 4096], P('replica', 'fsdp'), may hold values from -6 to 6
- w_gate: bfloat16 [4, 7168, 4096], P('replica', 'fsdp'), may hold values from -0.09375 to 0.09375
- w_up: bfloat16 [4, 7168, 4096], P('replica', 'fsdp'), may hold values from -0.09375 to 0.09375
- w_down: bfloat16 [4, 7168, 4096], P('replica', 'fsdp'), may hold values from -0.0625 to 0.0625
Outputs:
- grad_gate: bfloat16 [4, 7168, 4096], P('replica', 'fsdp')
- grad_up: bfloat16 [4, 7168, 4096], P('replica', 'fsdp')
- grad_down: bfloat16 [4, 7168, 4096], P('replica', 'fsdp')
The draws below stay inside these ranges and needn't reach their ends.
Inputs may be any that keep to these rules, and one draw needn't show every extreme that they name: partner is a permutation of the 4 replicas that forms one single cycle through all of them; no replica is its own partner.
All inputs are finite; a program needn't handle non-finite values.
Results may differ from the reference program's by a relative error of at most 0.025.
Values may be sent and summed in bfloat16 or wider, within the bound.
No kernel may reach another device: no remote copies, remote signals or barrier semaphores. Data moves between devices by JAX's collectives and lax.ppermute only.
A program may use at most 128 MiB of HBM per device.

```python
import math
import jax
import jax.numpy as jnp
from jax import lax

D = 4096
FFW = 7168
REPLICAS = 4
TOKENS = 128
BLOCKS = 8


def draw_partner(key, part):
    order = jax.random.permutation(jax.random.fold_in(key, 17), REPLICAS).astype(jnp.int32)
    following = jnp.roll(order, -1).astype(jnp.int32)
    result = jnp.zeros((REPLICAS,), jnp.int32).at[order].set(following)
    return result.astype(jnp.int32)


def level_of(own_key, extent, pieces, smallest, high):
    level = 1.0
    for position, shards_of in pieces:
        heights = jax.random.uniform(jax.random.fold_in(jax.random.fold_in(own_key, 6), position), (shards_of,), jnp.float32, smallest / len(pieces), high / len(pieces))
        level = level * jnp.repeat(jnp.exp(heights), extent[position] // shards_of).reshape((-1,) + (1,) * (len(extent) - 1 - position))
    return level


def centred(own_key, shape, spread, limit, cuts=(), dtype=jnp.bfloat16):
    drawn = jax.random.normal(own_key, shape, jnp.float32) * spread
    if len(cuts) > 0:
        drawn = level_of(own_key, shape, cuts, -0.22, 0.18) * drawn
    return jnp.clip(drawn, min=-limit, max=limit).astype(dtype)


def setup_inputs(seed: int = 0) -> dict:
    streams_of = jax.random.split(jax.random.key(seed), 6)
    return {
        "partner": draw_partner(jax.random.fold_in(streams_of[5], 71), 0),
        "tokens": centred(streams_of[1], (REPLICAS, TOKENS, D), 1.0, 6.0, ((0, 4), (1, 8))),
        "w_gate": centred(streams_of[2], (REPLICAS, FFW, D), D ** -0.5, 0.09375, ((0, 4), (1, 8))),
        "w_up": centred(streams_of[3], (REPLICAS, FFW, D), D ** -0.5, 0.09375, ((0, 4), (1, 8))),
        "w_down": centred(streams_of[4], (REPLICAS, FFW, D), FFW ** -0.5, 0.0625, ((0, 4), (1, 8))),
    }


def forward_pass(rows, gate_w, up_w, down_w):
    pre_gate = jnp.dot(rows, gate_w.T, preferred_element_type=jnp.float32)
    pre_up = jnp.dot(rows, up_w.T, preferred_element_type=jnp.float32)
    hidden = (jax.nn.silu(pre_gate) * pre_up).astype(jnp.bfloat16)
    width = FFW // BLOCKS
    hidden_blocks = hidden.reshape(TOKENS, BLOCKS, width).transpose(1, 0, 2)
    down_blocks = down_w.reshape(BLOCKS, width, D)

    def add_block(total, pair):
        term = jnp.dot(pair[0], pair[1], preferred_element_type=jnp.float32).astype(jnp.bfloat16)
        term = lax.optimization_barrier(term)
        return (total + term.astype(jnp.float32), None)
    output, _ = lax.scan(add_block, jnp.zeros((TOKENS, D), jnp.float32), (hidden_blocks, down_blocks))
    return (pre_gate, pre_up, hidden, output)

def reference(partner, tokens, w_gate, w_up, w_down):
    loss_scale = 1.0 / math.sqrt(TOKENS)
    gates_out = []
    ups_out = []
    downs_out = []
    for replica_id in range(REPLICAS):
        rows = tokens[replica_id]
        pre_gate, pre_up, hidden, student = forward_pass(rows, w_gate[replica_id], w_up[replica_id], w_down[replica_id])
        teacher_id = partner[replica_id]
        teacher_gate = jnp.take(w_gate, teacher_id, axis=0)
        teacher_up = jnp.take(w_up, teacher_id, axis=0)
        teacher_down = jnp.take(w_down, teacher_id, axis=0)
        teacher = forward_pass(rows, teacher_gate, teacher_up, teacher_down)[3]
        cotangent = ((student - teacher) * loss_scale).astype(jnp.bfloat16)
        grad_down = jnp.dot(hidden.T, cotangent, preferred_element_type=jnp.float32).astype(jnp.bfloat16)
        d_hidden = jnp.dot(cotangent, w_down[replica_id].T, preferred_element_type=jnp.float32)
        sigma = jax.nn.sigmoid(pre_gate)
        d_gate = (d_hidden * pre_up * sigma * (1.0 + pre_gate * (1.0 - sigma))).astype(jnp.bfloat16)
        d_up = (d_hidden * pre_gate * sigma).astype(jnp.bfloat16)
        grad_gate = jnp.dot(d_gate.T, rows, preferred_element_type=jnp.float32).astype(jnp.bfloat16)
        grad_up = jnp.dot(d_up.T, rows, preferred_element_type=jnp.float32).astype(jnp.bfloat16)
        gates_out.append(grad_gate)
        ups_out.append(grad_up)
        downs_out.append(grad_down)
    return (jnp.stack(gates_out), jnp.stack(ups_out), jnp.stack(downs_out))
```

```python
import math

import jax
import jax.numpy as jnp
from jax import lax
from jax.sharding import PartitionSpec as P


def peer(index, step, count):
    return index ^ step if count & (count - 1) == 0 else (index + step) % count


def fetch(value, axis, step, count, stride=1):
    pairs = [
        (peer(i, step, count) * stride + low, i * stride + low)
        for i in range(count)
        for low in range(stride)
    ]
    return lax.ppermute(value, axis, pairs)


def give(value, axis, step, count, stride=1):
    pairs = [
        (i * stride + low, peer(i, step, count) * stride + low)
        for i in range(count)
        for low in range(stride)
    ]
    return lax.ppermute(value, axis, pairs)


def swap(value, members):
    return lax.ppermute(value, "fsdp", [(i, i ^ 1) for i in range(members)])


def contract(left, right, left_dim, right_dim):
    return lax.dot_general(
        left, right, (((left_dim,), (right_dim,)), ((), ())), preferred_element_type=jnp.float32
    )


def gather_rows(rows, chips, members):
    mine = [rows] + [fetch(rows, "fsdp", k, chips, 2) for k in range(1, chips)]
    mine = jnp.concatenate(mine, axis=0)
    return jnp.concatenate([mine, swap(mine, members)], axis=0)


def scatter_rows(part, chips, members):
    half = part.shape[0] // 2
    rows = half // chips
    chip = part[:half] + swap(part[half:].astype(jnp.bfloat16), members).astype(jnp.float32)
    total = chip[:rows]
    for k in range(1, chips):
        piece = chip[k * rows : (k + 1) * rows].astype(jnp.bfloat16)
        total = total + give(piece, "fsdp", k, chips, 2).astype(jnp.float32)
    return total


def route(value, wanted, here, replicas):
    chosen = fetch(value, "replica", 1, replicas)
    for k in range(2, replicas):
        other = fetch(value, "replica", k, replicas)
        chosen = jnp.where(peer(here, k, replicas) == wanted, other, chosen)
    return chosen


def forward_pass(rows_all, gate_w, up_w, down_w):
    pre_gate = contract(gate_w, rows_all, 1, 1)
    pre_up = contract(up_w, rows_all, 1, 1)
    hidden = (jax.nn.silu(pre_gate) * pre_up).astype(jnp.bfloat16)
    partial_value = contract(hidden, down_w, 0, 0)
    return (pre_gate, pre_up, hidden, partial_value)


def local(partner, tokens, w_gate, w_up, w_down):
    rows = tokens[0]
    replicas = lax.axis_size("replica")
    members = lax.axis_size("fsdp")
    chips = members // 2
    here = lax.axis_index("replica")
    loss_scale = 1.0 / math.sqrt(rows.shape[0] * members)
    indices = jnp.arange(replicas, dtype=jnp.int32)
    taught = jnp.sum(jnp.where(partner == here, indices, 0))
    taught_by = jnp.sum(jnp.where(indices == here, partner, 0))
    foreign = route(rows, taught, here, replicas)
    rows_all = gather_rows(rows, chips, members)
    pre_gate, pre_up, hidden, student_part = forward_pass(rows_all, w_gate[0], w_up[0], w_down[0])
    foreign_all = gather_rows(foreign, chips, members)
    student = scatter_rows(student_part, chips, members)
    teacher_part = forward_pass(foreign_all, w_gate[0], w_up[0], w_down[0])[3]
    taught_sum = scatter_rows(teacher_part, chips, members)
    teacher = route(taught_sum.astype(jnp.bfloat16), taught_by, here, replicas).astype(jnp.float32)
    cotangent = ((student - teacher) * loss_scale).astype(jnp.bfloat16)
    cotangent_all = gather_rows(cotangent, chips, members)
    grad_down = contract(hidden, cotangent_all, 1, 0).astype(jnp.bfloat16)
    d_hidden = contract(w_down[0], cotangent_all, 1, 1)
    sigma = jax.nn.sigmoid(pre_gate)
    d_gate = (d_hidden * pre_up * sigma * (1.0 + pre_gate * (1.0 - sigma))).astype(jnp.bfloat16)
    d_up = (d_hidden * pre_gate * sigma).astype(jnp.bfloat16)
    grad_gate = contract(d_gate, rows_all, 1, 0).astype(jnp.bfloat16)
    grad_up = contract(d_up, rows_all, 1, 0).astype(jnp.bfloat16)
    return (grad_gate[None], grad_up[None], grad_down[None])


def solution(mesh):
    in_specs = (P(),) + (P("replica", "fsdp", None),) * 4
    out_specs = (P("replica", "fsdp", None),) * 3
    return jax.shard_map(local, mesh=mesh, in_specs=in_specs, out_specs=out_specs, check_vma=False)
```

```python
import functools
import math

import jax
import jax.numpy as jnp
from jax import lax
from jax.experimental import pallas as pl
from jax.experimental.pallas import tpu as pltpu
from jax.sharding import PartitionSpec as P


CHUNKS = 2
ANY = pl.BlockSpec(memory_space=pl.ANY)
VMEM = pl.BlockSpec(memory_space=pltpu.VMEM)


def peer(index, step, count):
    return index ^ step if count & (count - 1) == 0 else (index + step) % count


def fetch(value, axis, step, count, stride=1):
    pairs = [
        (peer(i, step, count) * stride + low, i * stride + low)
        for i in range(count)
        for low in range(stride)
    ]
    return lax.ppermute(value, axis, pairs)


def give(value, axis, step, count, stride=1):
    pairs = [
        (i * stride + low, peer(i, step, count) * stride + low)
        for i in range(count)
        for low in range(stride)
    ]
    return lax.ppermute(value, axis, pairs)


def swap(value, members):
    return lax.ppermute(value, "fsdp", [(i, i ^ 1) for i in range(members)])


def gather_rows(rows, chips, members):
    mine = [rows] + [fetch(rows, "fsdp", k, chips, 2) for k in range(1, chips)]
    return mine + [swap(piece, members) for piece in mine]


def scatter_rows(mine, theirs, chips, members):
    other = swap(theirs, members)
    rows, wide = mine.shape[0] // chips, mine.shape[1]
    terms = small_call(
        chip_kernel,
        [mine, other],
        [jax.ShapeDtypeStruct((rows, wide), jnp.float32)]
        + [jax.ShapeDtypeStruct((rows, wide), jnp.bfloat16)] * (chips - 1),
    )
    return [terms[0]] + [give(terms[k], "fsdp", k, chips, 2) for k in range(1, chips)]


def spread(value, replicas):
    return [fetch(value, "replica", k, replicas) for k in range(1, replicas)]


def small_call(kernel, operands, shapes, partner=None):
    head = [] if partner is None else [partner]
    flat = shapes if isinstance(shapes, list) else [shapes]
    size = sum(x.size for x in operands) + sum(x.size for x in flat)
    return pl.pallas_call(
        kernel,
        out_shape=shapes,
        in_specs=[pl.BlockSpec(memory_space=pltpu.SMEM)] * len(head) + [VMEM] * len(operands),
        out_specs=[VMEM] * len(flat) if isinstance(shapes, list) else VMEM,
        compiler_params=pltpu.CompilerParams(vmem_limit_bytes=4 << 20),
        cost_estimate=pl.CostEstimate(flops=size, bytes_accessed=2 * size, transcendentals=0),
    )(*head, *operands)


def chip_kernel(mine, other, own, *pieces):
    rows = own.shape[0]
    for k, target in enumerate((own,) + pieces):
        part = pl.ds(k * rows, rows)
        target[...] = (mine[part] + other[part].astype(jnp.float32)).astype(target.dtype)


def sum_kernel(*refs):
    total = refs[0][...]
    for term in refs[1:-1]:
        total = total + term[...].astype(jnp.float32)
    refs[-1][...] = total.astype(refs[-1].dtype)


def choose(candidates, step):
    chosen = candidates[0][...]
    for k in range(1, len(candidates)):
        chosen = jnp.where(step == k + 1, candidates[k][...], chosen)
    return chosen


def step_to(wanted, here, replicas):
    return here ^ wanted if replicas & (replicas - 1) == 0 else (wanted - here + replicas) % replicas


def foreign_kernel(partner, *refs):
    replicas = partner.shape[0]
    here = lax.axis_index("replica")
    taught = sum(jnp.where(partner[r] == here, r, 0) for r in range(replicas))
    refs[-1][...] = choose(refs[:-1], step_to(taught, here, replicas))


def cotangent_kernel(chips, start, scale, partner, *refs):
    replicas = partner.shape[0]
    here = lax.axis_index("replica")
    wanted = sum(jnp.where(here == r, partner[r], 0) for r in range(replicas))
    target = refs[-1]
    columns = pl.ds(start, target.shape[1])
    student = refs[0][:, columns]
    for term in refs[1:chips]:
        student = student + term[:, columns].astype(jnp.float32)
    teacher = choose(refs[chips:-1], step_to(wanted, here, replicas)).astype(jnp.float32)
    target[...] = ((student - teacher) * scale).astype(target.dtype)


def contract(left, right, left_dim, right_dim):
    return lax.dot_general(
        left, right, (((left_dim,), (right_dim,)), ((), ())), preferred_element_type=jnp.float32
    )


def block_of(count):
    return 128 if count % 128 == 0 else count


def put_together(pieces, whole):
    rows = pieces[0].shape[0]
    for i, piece in enumerate(pieces):
        whole[i * rows : (i + 1) * rows, :] = piece[...]


def load_kernel(*refs):
    count = len(refs) // 2
    sems = refs[-1]
    copies = [
        pltpu.make_async_copy(refs[i], refs[count + i], sems.at[i]) for i in range(count)
    ]
    for copy in copies:
        copy.start()
    for copy in copies:
        copy.wait()


def in_hbm(array):
    return pltpu.with_memory_space_constraint(array, pltpu.HBM)


def in_vmem(array):
    return pltpu.with_memory_space_constraint(array, pltpu.VMEM)


def load(*weights):
    return pl.pallas_call(
        load_kernel,
        out_shape=[pltpu.VMEM(w.shape, w.dtype) for w in weights],
        in_specs=[ANY] * len(weights),
        out_specs=[VMEM] * len(weights),
        scratch_shapes=[pltpu.SemaphoreType.DMA((len(weights),))],
        compiler_params=pltpu.CompilerParams(vmem_limit_bytes=1 << 20),
        cost_estimate=pl.CostEstimate(
            flops=0, bytes_accessed=sum(2 * w.size for w in weights), transcendentals=0
        ),
        name="load",
    )(*[in_hbm(w) for w in weights])


def forward_kernel(count, chunks, keep, *refs):
    pieces, (gate_w, up_w, down_w) = refs[:count], refs[count : count + 3]
    rest = list(refs[count + 3 :])
    if keep:
        down_hbm = down_w
        down_w, rows_all, pre_gate, pre_up, hidden = rest[:5]
        outs, sem = rest[5:-1], rest[-1]
        fill = pltpu.make_async_copy(down_hbm, down_w, sem)
        fill.start()
    else:
        outs, (rows_all, hidden) = rest[: 2 * chunks], rest[2 * chunks :]
    height = gate_w.shape[0]
    step = block_of(height)
    put_together(pieces, rows_all)
    for j in range(height // step):
        part = pl.ds(j * step, step)
        gate = contract(gate_w[part], rows_all[...], 1, 1)
        up = contract(up_w[part], rows_all[...], 1, 1)
        if keep:
            pre_gate[part] = gate
            pre_up[part] = up
        hidden[part] = (gate * jax.nn.sigmoid(gate) * up).astype(hidden.dtype)
    if keep:
        fill.wait()
    half = rows_all.shape[0] // 2
    wide = down_w.shape[1] // chunks
    tile = min(512, wide)
    across = hidden[...].T
    for c in range(chunks):
        for start in range(0, wide, tile):
            value = contract(across, down_w[:, pl.ds(c * wide + start, tile)], 1, 0)
            outs[2 * c][:, start : start + tile] = value[:half]
            outs[2 * c + 1][:, start : start + tile] = value[half:].astype(jnp.bfloat16)


def forward(pieces, gate_w, up_w, down_w, chunks, keep):
    height, depth = gate_w.shape
    rows = len(pieces) * pieces[0].shape[0]
    wide = depth // chunks
    shapes, scratch = [], []
    if keep:
        scratch += [pltpu.SemaphoreType.DMA]
        shapes += [
            pltpu.VMEM((height, depth), jnp.bfloat16),
            jax.ShapeDtypeStruct((rows, depth), jnp.bfloat16),
            jax.ShapeDtypeStruct((height, rows), jnp.float32),
            jax.ShapeDtypeStruct((height, rows), jnp.float32),
            jax.ShapeDtypeStruct((height, rows), jnp.bfloat16),
        ]
    else:
        scratch += [pltpu.VMEM((rows, depth), jnp.bfloat16), pltpu.VMEM((height, rows), jnp.bfloat16)]
    for _ in range(chunks):
        shapes.append(jax.ShapeDtypeStruct((rows // 2, wide), jnp.float32))
        shapes.append(jax.ShapeDtypeStruct((rows // 2, wide), jnp.bfloat16))
    return pl.pallas_call(
        functools.partial(forward_kernel, len(pieces), chunks, keep),
        out_shape=shapes,
        in_specs=[VMEM] * (len(pieces) + 2) + [ANY if keep else VMEM],
        out_specs=[VMEM] * len(shapes),
        scratch_shapes=scratch,
        compiler_params=pltpu.CompilerParams(vmem_limit_bytes=12 << 20),
        cost_estimate=pl.CostEstimate(
            flops=6 * rows * height * depth,
            bytes_accessed=6 * height * depth,
            transcendentals=rows * height,
        ),
        name="student_forward" if keep else "teacher_forward",
    )(*pieces, in_vmem(gate_w), in_vmem(up_w), (in_hbm if keep else in_vmem)(down_w))


def backward_kernel(count, first, final, start, *refs):
    pieces, refs = refs[:count], list(refs[count:])
    hidden, down_w = refs[:2]
    refs = refs[2:]
    if not first:
        before = refs[0]
        refs = refs[2:]
    if final:
        pre_gate, pre_up, rows_all = refs[:3]
        refs = refs[3:]
        grad_down, grad_gate, grad_up = refs[:3]
        refs = refs[3:]
        cotangent, stage_down, stage_gate, stage_up, sems = refs
    else:
        grad_down, after = refs[:2]
        cotangent, stage_down, sems = refs[2:]
    height = hidden.shape[0]
    wide = cotangent.shape[1]
    columns = pl.ds(start, wide)
    step = block_of(height)
    blocks = height // step
    put_together(pieces, cotangent)
    copies = []

    def send(source, target):
        copies.append(pltpu.make_async_copy(source, target, sems.at[len(copies)]))
        copies[-1].start()

    for j in range(blocks):
        part = pl.ds(j * step, step)
        stage_down[part] = contract(hidden[part], cotangent[...], 1, 0).astype(jnp.bfloat16)
        send(stage_down.at[part], grad_down.at[part, columns])
    for j in range(blocks):
        part = pl.ds(j * step, step)
        d_hidden = contract(down_w[part, columns], cotangent[...], 1, 1)
        if not first:
            d_hidden = d_hidden + before[part]
        if not final:
            after[part] = d_hidden
            continue
        gate, up = pre_gate[part], pre_up[part]
        sigma = jax.nn.sigmoid(gate)
        d_gate = (d_hidden * up * sigma * (1.0 + gate * (1.0 - sigma))).astype(jnp.bfloat16)
        d_up = (d_hidden * gate * sigma).astype(jnp.bfloat16)
        stage_gate[part] = contract(d_gate, rows_all[...], 1, 0).astype(jnp.bfloat16)
        send(stage_gate.at[part], grad_gate.at[part])
        stage_up[part] = contract(d_up, rows_all[...], 1, 0).astype(jnp.bfloat16)
        send(stage_up.at[part], grad_up.at[part])
    for copy in copies:
        copy.wait()


def backward(pieces, hidden, down_w, carried, saved, start):
    height, depth = down_w.shape
    rows = hidden.shape[1]
    wide = pieces[0].shape[1]
    blocks = height // block_of(height)
    first, final = carried is None, saved is not None
    operands = list(pieces) + [hidden, in_vmem(down_w)]
    in_specs = [VMEM] * (len(pieces) + 2)
    aliases = {}
    if not first:
        aliases = {len(operands) + 1: 0}
        operands += [carried[0], in_hbm(carried[1])]
        in_specs += [VMEM, ANY]
    whole = jax.ShapeDtypeStruct((height, depth), jnp.bfloat16)
    scratch = [
        pltpu.VMEM((rows, wide), jnp.bfloat16),
        pltpu.VMEM((height, wide), jnp.bfloat16),
    ]
    sends = blocks
    if final:
        operands += list(saved)
        in_specs += [VMEM] * 3
        shapes, out_specs = [whole] * 3, [ANY] * 3
        scratch += [pltpu.VMEM((height, depth), jnp.bfloat16)] * 2
        sends = 3 * blocks
    else:
        shapes = [whole, jax.ShapeDtypeStruct((height, rows), jnp.float32)]
        out_specs = [ANY, VMEM]
    scratch += [pltpu.SemaphoreType.DMA((sends,))]
    products = 4 * wide + (4 * depth if final else 0)
    return pl.pallas_call(
        functools.partial(backward_kernel, len(pieces), first, final, start),
        out_shape=shapes,
        in_specs=in_specs,
        out_specs=out_specs,
        scratch_shapes=scratch,
        input_output_aliases=aliases,
        compiler_params=pltpu.CompilerParams(vmem_limit_bytes=(26 if final else 8) << 20),
        cost_estimate=pl.CostEstimate(
            flops=products * rows * height,
            bytes_accessed=products * height,
            transcendentals=rows * height if final else 0,
        ),
    )(*operands)


def local(partner, tokens, w_gate, w_up, w_down):
    rows = tokens[0]
    gate_w, up_w, down_w = w_gate[0], w_up[0], w_down[0]
    replicas = lax.axis_size("replica")
    members = lax.axis_size("fsdp")
    chips = members // 2
    scale = 1.0 / math.sqrt(rows.shape[0] * members)
    foreign = small_call(
        foreign_kernel,
        spread(rows, replicas),
        jax.ShapeDtypeStruct(rows.shape, rows.dtype),
        partner,
    )
    gate_w, up_w = load(gate_w, up_w)
    own_pieces = gather_rows(rows, chips, members)
    down_w, rows_all, pre_gate, pre_up, hidden, mine, theirs = forward(
        own_pieces, gate_w, up_w, down_w, 1, True
    )
    student = scatter_rows(mine, theirs, chips, members)
    foreign_pieces = gather_rows(foreign, chips, members)
    parts = forward(foreign_pieces, gate_w, up_w, down_w, CHUNKS, False)
    wide = rows.shape[1] // CHUNKS
    part = jax.ShapeDtypeStruct((rows.shape[0], wide), jnp.bfloat16)
    carried = None
    for c in range(CHUNKS):
        terms = scatter_rows(parts[2 * c], parts[2 * c + 1], chips, members)
        taught = small_call(sum_kernel, terms, part)
        cotangent = small_call(
            functools.partial(cotangent_kernel, chips, c * wide, scale),
            student + spread(taught, replicas),
            part,
            partner,
        )
        pieces = gather_rows(cotangent, chips, members)
        saved = (pre_gate, pre_up, rows_all) if c == CHUNKS - 1 else None
        grads = backward(pieces, hidden, down_w, carried, saved, c * wide)
        carried = (grads[1], grads[0])
    grad_down, grad_gate, grad_up = grads
    return (grad_gate[None], grad_up[None], grad_down[None])


def solution(mesh):
    in_specs = (P(),) + (P("replica", "fsdp", None),) * 4
    out_specs = (P("replica", "fsdp", None),) * 3
    return jax.shard_map(local, mesh=mesh, in_specs=in_specs, out_specs=out_specs, check_vma=False)
```

```python
import functools
import math

import jax
import jax.numpy as jnp
from jax import lax
from jax.experimental import pallas as pl
from jax.experimental.pallas import tpu as pltpu
from jax.sharding import PartitionSpec as P


CHUNKS = 2
ANY = pl.BlockSpec(memory_space=pl.ANY)
VMEM = pl.BlockSpec(memory_space=pltpu.VMEM)


def exchange(value, axis, step, stride, count):
    pairs = [
        ((i ^ step) * stride + low, i * stride + low) for i in range(count) for low in range(stride)
    ]
    return lax.ppermute(value, axis, pairs)


def levels(count):
    assert count & (count - 1) == 0
    return [1 << level for level in range(count.bit_length() - 1)]


def arrangement(count):
    order = [0]
    for step in levels(count)[::-1]:
        order += [held + step for held in order]
    return order


def swap(value, members):
    return lax.ppermute(value, "fsdp", [(i, i ^ 1) for i in range(members)])


def gather_rows(rows, chips, members, relay=False):
    mine, theirs = [rows], []
    for step in arrangement(chips)[1:] if not relay else []:
        mine.append(exchange(rows, "fsdp", step, 2, chips))
    for step in levels(chips)[::-1] if relay else []:
        fresh = []
        for piece in mine:
            fresh.append(exchange(piece, "fsdp", step, 2, chips))
        mine += fresh
    for step, piece in zip(arrangement(chips), mine):
        theirs.append(swap(piece, members))
    return mine + theirs


def chip_sum(mine, theirs, chips, kept, members):
    other = swap(theirs, members)
    rows, wide = mine.shape[0] // chips, mine.shape[1]
    part = jax.ShapeDtypeStruct((rows, wide), jnp.bfloat16)
    return small_call(
        chip_kernel,
        [mine, other],
        [jax.ShapeDtypeStruct((rows, wide), jnp.float32)] * kept + [part] * (chips - kept),
    )


def scatter_rows(mine, theirs, chips, members):
    terms = list(chip_sum(mine, theirs, chips, 1, members))
    for i, step in enumerate(arrangement(chips)[1:]):
        terms[i + 1] = exchange(terms[i + 1], "fsdp", step, 2, chips)
    return terms


def scatter_halving(mine, theirs, chips, members):
    first = chip_sum(mine, theirs, chips, chips // 2, members)
    part = jax.ShapeDtypeStruct(first[0].shape, jnp.bfloat16)
    terms = [[term] for term in first]
    for step in levels(chips):
        kept = len(terms) // 2
        for i in reversed(range(kept)):
            sent = terms[kept + i]
            if len(sent) > 1:
                sent = [small_call(sum_kernel, sent, part)]
            terms[i].append(exchange(sent[0], "fsdp", step, 2, chips))
        terms = terms[:kept]
    return terms[0]


def spread(value, replicas):
    others = []
    for step in range(1, replicas):
        others.append(exchange(value, "replica", step, 1, replicas))
    return others


def small_call(kernel, operands, shapes, partner=None):
    head = [] if partner is None else [partner]
    flat = shapes if isinstance(shapes, list) else [shapes]
    size = sum(x.size for x in operands) + sum(x.size for x in flat)
    return pl.pallas_call(
        kernel,
        out_shape=shapes,
        in_specs=[pl.BlockSpec(memory_space=pltpu.SMEM)] * len(head) + [VMEM] * len(operands),
        out_specs=[VMEM] * len(flat) if isinstance(shapes, list) else VMEM,
        compiler_params=pltpu.CompilerParams(vmem_limit_bytes=4 << 20),
        cost_estimate=pl.CostEstimate(flops=size, bytes_accessed=2 * size, transcendentals=0),
    )(*head, *operands)


def chip_kernel(mine, other, own, *pieces):
    rows = own.shape[0]
    for k, target in enumerate((own,) + pieces):
        part = pl.ds(k * rows, rows)
        target[...] = (mine[part] + other[part].astype(jnp.float32)).astype(target.dtype)


def sum_kernel(*refs):
    total = refs[0][...]
    for term in refs[1:-1]:
        total = total + term[...].astype(jnp.float32)
    refs[-1][...] = total.astype(refs[-1].dtype)


def choose(candidates, step):
    chosen = candidates[0][...]
    for k in range(1, len(candidates)):
        chosen = jnp.where(step == k + 1, candidates[k][...], chosen)
    return chosen


def foreign_kernel(partner, *refs):
    replicas = partner.shape[0]
    here = lax.axis_index("replica")
    taught = sum(jnp.where(partner[r] == here, r, 0) for r in range(replicas))
    refs[-1][...] = choose(refs[:-1], here ^ taught)


def cotangent_kernel(count, start, scale, partner, *refs):
    replicas = partner.shape[0]
    here = lax.axis_index("replica")
    wanted = sum(jnp.where(here == r, partner[r], 0) for r in range(replicas))
    target = refs[-1]
    columns = pl.ds(start, target.shape[1])
    student = refs[0][:, columns]
    for term in refs[1:count]:
        student = student + term[:, columns].astype(jnp.float32)
    teacher = choose(refs[count:-1], here ^ wanted).astype(jnp.float32)
    target[...] = ((student - teacher) * scale).astype(target.dtype)


def contract(left, right, left_dim, right_dim):
    return lax.dot_general(
        left, right, (((left_dim,), (right_dim,)), ((), ())), preferred_element_type=jnp.float32
    )


def block_of(count):
    return 128 if count % 128 == 0 else count


def put_together(pieces, whole):
    rows = pieces[0].shape[0]
    for i, piece in enumerate(pieces):
        whole[i * rows : (i + 1) * rows, :] = piece[...]


def load_kernel(*refs):
    count = len(refs) // 2
    sems = refs[-1]
    copies = [
        pltpu.make_async_copy(refs[i], refs[count + i], sems.at[i]) for i in range(count)
    ]
    for copy in copies:
        copy.start()
    for copy in copies:
        copy.wait()


def in_hbm(array):
    return pltpu.with_memory_space_constraint(array, pltpu.HBM)


def in_vmem(array):
    return pltpu.with_memory_space_constraint(array, pltpu.VMEM)


def load(*weights):
    return pl.pallas_call(
        load_kernel,
        out_shape=[pltpu.VMEM(w.shape, w.dtype) for w in weights],
        in_specs=[ANY] * len(weights),
        out_specs=[VMEM] * len(weights),
        scratch_shapes=[pltpu.SemaphoreType.DMA((len(weights),))],
        compiler_params=pltpu.CompilerParams(vmem_limit_bytes=1 << 20),
        cost_estimate=pl.CostEstimate(
            flops=0, bytes_accessed=sum(2 * w.size for w in weights), transcendentals=0
        ),
        name="load",
    )(*[in_hbm(w) for w in weights])


def forward_kernel(count, chunks, keep, *refs):
    pieces, (gate_w, up_w, down_w) = refs[:count], refs[count : count + 3]
    rest = list(refs[count + 3 :])
    if keep:
        down_hbm = down_w
        down_w, rows_all, pre_gate, pre_up, hidden = rest[:5]
        outs, sem = rest[5:-1], rest[-1]
        fill = pltpu.make_async_copy(down_hbm, down_w, sem)
        fill.start()
    else:
        outs, (rows_all, hidden) = rest[: 2 * chunks], rest[2 * chunks :]
    height = gate_w.shape[0]
    step = block_of(height)
    put_together(pieces, rows_all)
    for j in range(height // step):
        part = pl.ds(j * step, step)
        gate = contract(gate_w[part], rows_all[...], 1, 1)
        up = contract(up_w[part], rows_all[...], 1, 1)
        if keep:
            pre_gate[part] = gate
            pre_up[part] = up
        hidden[part] = (gate * jax.nn.sigmoid(gate) * up).astype(hidden.dtype)
    if keep:
        fill.wait()
    half = rows_all.shape[0] // 2
    wide = down_w.shape[1] // chunks
    tile = min(512, wide)
    across = hidden[...].T
    for c in range(chunks):
        for start in range(0, wide, tile):
            value = contract(across, down_w[:, pl.ds(c * wide + start, tile)], 1, 0)
            outs[2 * c][:, start : start + tile] = value[:half]
            outs[2 * c + 1][:, start : start + tile] = value[half:].astype(jnp.bfloat16)


def forward(pieces, gate_w, up_w, down_w, chunks, keep):
    height, depth = gate_w.shape
    rows = len(pieces) * pieces[0].shape[0]
    wide = depth // chunks
    shapes, scratch = [], []
    if keep:
        scratch += [pltpu.SemaphoreType.DMA]
        shapes += [
            pltpu.VMEM((height, depth), jnp.bfloat16),
            jax.ShapeDtypeStruct((rows, depth), jnp.bfloat16),
            jax.ShapeDtypeStruct((height, rows), jnp.float32),
            jax.ShapeDtypeStruct((height, rows), jnp.float32),
            jax.ShapeDtypeStruct((height, rows), jnp.bfloat16),
        ]
    else:
        scratch += [pltpu.VMEM((rows, depth), jnp.bfloat16), pltpu.VMEM((height, rows), jnp.bfloat16)]
    for _ in range(chunks):
        shapes.append(jax.ShapeDtypeStruct((rows // 2, wide), jnp.float32))
        shapes.append(jax.ShapeDtypeStruct((rows // 2, wide), jnp.bfloat16))
    return pl.pallas_call(
        functools.partial(forward_kernel, len(pieces), chunks, keep),
        out_shape=shapes,
        in_specs=[VMEM] * (len(pieces) + 2) + [ANY if keep else VMEM],
        out_specs=[VMEM] * len(shapes),
        scratch_shapes=scratch,
        compiler_params=pltpu.CompilerParams(vmem_limit_bytes=12 << 20),
        cost_estimate=pl.CostEstimate(
            flops=6 * rows * height * depth,
            bytes_accessed=6 * height * depth,
            transcendentals=rows * height,
        ),
        name="student_forward" if keep else "teacher_forward",
    )(*pieces, in_vmem(gate_w), in_vmem(up_w), (in_hbm if keep else in_vmem)(down_w))


def backward_kernel(count, first, final, start, *refs):
    pieces, refs = refs[:count], list(refs[count:])
    hidden, down_w = refs[:2]
    refs = refs[2:]
    if not first:
        before = refs[0]
        refs = refs[2:]
    if final:
        pre_gate, pre_up, rows_all = refs[:3]
        refs = refs[3:]
        grad_down, grad_gate, grad_up = refs[:3]
        refs = refs[3:]
        cotangent, stage_down, stage_gate, stage_up, sems = refs
    else:
        grad_down, after = refs[:2]
        cotangent, stage_down, sems = refs[2:]
    height = hidden.shape[0]
    wide = cotangent.shape[1]
    columns = pl.ds(start, wide)
    step = block_of(height)
    blocks = height // step
    put_together(pieces, cotangent)
    copies = []

    def send(source, target):
        copies.append(pltpu.make_async_copy(source, target, sems.at[len(copies)]))
        copies[-1].start()

    for j in range(blocks):
        part = pl.ds(j * step, step)
        stage_down[part] = contract(hidden[part], cotangent[...], 1, 0).astype(jnp.bfloat16)
        send(stage_down.at[part], grad_down.at[part, columns])
    for j in range(blocks):
        part = pl.ds(j * step, step)
        d_hidden = contract(down_w[part, columns], cotangent[...], 1, 1)
        if not first:
            d_hidden = d_hidden + before[part]
        if not final:
            after[part] = d_hidden
            continue
        gate, up = pre_gate[part], pre_up[part]
        sigma = jax.nn.sigmoid(gate)
        d_gate = (d_hidden * up * sigma * (1.0 + gate * (1.0 - sigma))).astype(jnp.bfloat16)
        d_up = (d_hidden * gate * sigma).astype(jnp.bfloat16)
        stage_gate[part] = contract(d_gate, rows_all[...], 1, 0).astype(jnp.bfloat16)
        send(stage_gate.at[part], grad_gate.at[part])
        stage_up[part] = contract(d_up, rows_all[...], 1, 0).astype(jnp.bfloat16)
        send(stage_up.at[part], grad_up.at[part])
    for copy in copies:
        copy.wait()


def backward(pieces, hidden, down_w, carried, saved, start):
    height, depth = down_w.shape
    rows = hidden.shape[1]
    wide = pieces[0].shape[1]
    blocks = height // block_of(height)
    first, final = carried is None, saved is not None
    operands = list(pieces) + [hidden, in_vmem(down_w)]
    in_specs = [VMEM] * (len(pieces) + 2)
    aliases = {}
    if not first:
        aliases = {len(operands) + 1: 0}
        operands += [carried[0], in_hbm(carried[1])]
        in_specs += [VMEM, ANY]
    whole = jax.ShapeDtypeStruct((height, depth), jnp.bfloat16)
    scratch = [
        pltpu.VMEM((rows, wide), jnp.bfloat16),
        pltpu.VMEM((height, wide), jnp.bfloat16),
    ]
    sends = blocks
    if final:
        operands += list(saved)
        in_specs += [VMEM] * 3
        shapes, out_specs = [whole] * 3, [ANY] * 3
        scratch += [pltpu.VMEM((height, depth), jnp.bfloat16)] * 2
        sends = 3 * blocks
    else:
        shapes = [whole, jax.ShapeDtypeStruct((height, rows), jnp.float32)]
        out_specs = [ANY, VMEM]
    scratch += [pltpu.SemaphoreType.DMA((sends,))]
    products = 4 * wide + (4 * depth if final else 0)
    return pl.pallas_call(
        functools.partial(backward_kernel, len(pieces), first, final, start),
        out_shape=shapes,
        in_specs=in_specs,
        out_specs=out_specs,
        scratch_shapes=scratch,
        input_output_aliases=aliases,
        compiler_params=pltpu.CompilerParams(vmem_limit_bytes=(26 if final else 8) << 20),
        cost_estimate=pl.CostEstimate(
            flops=products * rows * height,
            bytes_accessed=products * height,
            transcendentals=rows * height if final else 0,
        ),
    )(*operands)


def local(partner, tokens, w_gate, w_up, w_down):
    rows = tokens[0]
    gate_w, up_w, down_w = w_gate[0], w_up[0], w_down[0]
    replicas = lax.axis_size("replica")
    members = lax.axis_size("fsdp")
    chips = members // 2
    scale = 1.0 / math.sqrt(rows.shape[0] * members)
    foreign = small_call(
        foreign_kernel,
        spread(rows, replicas),
        jax.ShapeDtypeStruct(rows.shape, rows.dtype),
        partner,
    )
    gate_w, up_w = load(gate_w, up_w)
    own_pieces = gather_rows(rows, chips, members, relay=True)
    down_w, rows_all, pre_gate, pre_up, hidden, mine, theirs = forward(
        own_pieces, gate_w, up_w, down_w, 1, True
    )
    student = scatter_halving(mine, theirs, chips, members)
    foreign_pieces = gather_rows(foreign, chips, members)
    parts = forward(foreign_pieces, gate_w, up_w, down_w, CHUNKS, False)
    wide = rows.shape[1] // CHUNKS
    part = jax.ShapeDtypeStruct((rows.shape[0], wide), jnp.bfloat16)
    carried = None
    for c in range(CHUNKS):
        terms = scatter_rows(parts[2 * c], parts[2 * c + 1], chips, members)
        taught = small_call(sum_kernel, terms, part)
        cotangent = small_call(
            functools.partial(cotangent_kernel, len(student), c * wide, scale),
            student + spread(taught, replicas),
            part,
            partner,
        )
        pieces = gather_rows(cotangent, chips, members)
        saved = (pre_gate, pre_up, rows_all) if c == CHUNKS - 1 else None
        grads = backward(pieces, hidden, down_w, carried, saved, c * wide)
        carried = (grads[1], grads[0])
    grad_down, grad_gate, grad_up = grads
    return (grad_gate[None], grad_up[None], grad_down[None])


def solution(mesh):
    in_specs = (P(),) + (P("replica", "fsdp", None),) * 4
    out_specs = (P("replica", "fsdp", None),) * 3
    return jax.shard_map(local, mesh=mesh, in_specs=in_specs, out_specs=out_specs, check_vma=False)
```

```python
import functools
import math

import jax
import jax.numpy as jnp
from jax import lax
from jax.experimental import pallas as pl
from jax.experimental.pallas import tpu as pltpu
from jax.sharding import PartitionSpec as P


CHUNKS = 2
ANY = pl.BlockSpec(memory_space=pl.ANY)
VMEM = pl.BlockSpec(memory_space=pltpu.VMEM)


def exchange(value, axis, step, stride, count):
    pairs = [
        ((i ^ step) * stride + low, i * stride + low) for i in range(count) for low in range(stride)
    ]
    return lax.ppermute(value, axis, pairs)


def levels(count):
    assert count & (count - 1) == 0
    return [1 << level for level in range(count.bit_length() - 1)]


def arrangement(count):
    order = [0]
    for step in levels(count)[::-1]:
        order += [held + step for held in order]
    return order


def swap(value, members):
    return lax.ppermute(value, "fsdp", [(i, i ^ 1) for i in range(members)])


def gather_direct(rows, chips):
    mine = [rows]
    for step in arrangement(chips)[1:]:
        mine.append(exchange(rows, "fsdp", step, 2, chips))
    return mine


def gather_doubling(rows, chips):
    mine = [rows]
    for step in levels(chips)[::-1]:
        fresh = []
        for piece in mine:
            fresh.append(exchange(piece, "fsdp", step, 2, chips))
        mine += fresh
    return mine


def with_other_core(mine, members):
    theirs = []
    for piece in mine:
        theirs.append(swap(piece, members))
    return mine + theirs


def chip_sum(mine, theirs, chips, kept, members):
    other = swap(theirs, members)
    rows, wide = mine.shape[0] // chips, mine.shape[1]
    part = jax.ShapeDtypeStruct((rows, wide), jnp.bfloat16)
    return small_call(
        chip_kernel,
        [mine, other],
        [jax.ShapeDtypeStruct((rows, wide), jnp.float32)] * kept + [part] * (chips - kept),
    )


def scatter_direct(mine, theirs, chips, members):
    terms = list(chip_sum(mine, theirs, chips, 1, members))
    for i, step in enumerate(arrangement(chips)[1:]):
        terms[i + 1] = exchange(terms[i + 1], "fsdp", step, 2, chips)
    return terms


def scatter_halving(mine, theirs, chips, members):
    first = chip_sum(mine, theirs, chips, chips // 2, members)
    part = jax.ShapeDtypeStruct(first[0].shape, jnp.bfloat16)
    terms = [[term] for term in first]
    for step in levels(chips):
        kept = len(terms) // 2
        for i in reversed(range(kept)):
            sent = terms[kept + i]
            if len(sent) > 1:
                sent = [small_call(sum_kernel, sent, part)]
            terms[i].append(exchange(sent[0], "fsdp", step, 2, chips))
        terms = terms[:kept]
    return terms[0]


def spread(value, replicas):
    others = []
    for step in range(1, replicas):
        others.append(exchange(value, "replica", step, 1, replicas))
    return others


def small_call(kernel, operands, shapes, partner=None):
    head = [] if partner is None else [partner]
    flat = shapes if isinstance(shapes, list) else [shapes]
    size = sum(x.size for x in operands) + sum(x.size for x in flat)
    return pl.pallas_call(
        kernel,
        out_shape=shapes,
        in_specs=[pl.BlockSpec(memory_space=pltpu.SMEM)] * len(head) + [VMEM] * len(operands),
        out_specs=[VMEM] * len(flat) if isinstance(shapes, list) else VMEM,
        compiler_params=pltpu.CompilerParams(vmem_limit_bytes=4 << 20),
        cost_estimate=pl.CostEstimate(flops=size, bytes_accessed=2 * size, transcendentals=0),
    )(*head, *operands)


def chip_kernel(mine, other, own, *pieces):
    rows = own.shape[0]
    for k, target in enumerate((own,) + pieces):
        part = pl.ds(k * rows, rows)
        target[...] = (mine[part] + other[part].astype(jnp.float32)).astype(target.dtype)


def sum_kernel(*refs):
    total = refs[0][...]
    for term in refs[1:-1]:
        total = total + term[...].astype(jnp.float32)
    refs[-1][...] = total.astype(refs[-1].dtype)


def choose(candidates, step):
    chosen = candidates[0][...]
    for k in range(1, len(candidates)):
        chosen = jnp.where(step == k + 1, candidates[k][...], chosen)
    return chosen


def foreign_kernel(partner, *refs):
    replicas = partner.shape[0]
    here = lax.axis_index("replica")
    taught = sum(jnp.where(partner[r] == here, r, 0) for r in range(replicas))
    refs[-1][...] = choose(refs[:-1], here ^ taught)


def cotangent_kernel(count, start, scale, partner, *refs):
    replicas = partner.shape[0]
    here = lax.axis_index("replica")
    wanted = sum(jnp.where(here == r, partner[r], 0) for r in range(replicas))
    target = refs[-1]
    columns = pl.ds(start, target.shape[1])
    student = refs[0][:, columns]
    for term in refs[1:count]:
        student = student + term[:, columns].astype(jnp.float32)
    teacher = choose(refs[count:-1], here ^ wanted).astype(jnp.float32)
    target[...] = ((student - teacher) * scale).astype(target.dtype)


def contract(left, right, left_dim, right_dim):
    return lax.dot_general(
        left, right, (((left_dim,), (right_dim,)), ((), ())), preferred_element_type=jnp.float32
    )


def block_of(count):
    return 128 if count % 128 == 0 else count


def put_together(pieces, whole):
    rows = pieces[0].shape[0]
    for i, piece in enumerate(pieces):
        whole[i * rows : (i + 1) * rows, :] = piece[...]


def load_kernel(*refs):
    count = len(refs) // 2
    sems = refs[-1]
    copies = [
        pltpu.make_async_copy(refs[i], refs[count + i], sems.at[i]) for i in range(count)
    ]
    for copy in copies:
        copy.start()
    for copy in copies:
        copy.wait()


def in_hbm(array):
    return pltpu.with_memory_space_constraint(array, pltpu.HBM)


def in_vmem(array):
    return pltpu.with_memory_space_constraint(array, pltpu.VMEM)


def load(*weights):
    return pl.pallas_call(
        load_kernel,
        out_shape=[pltpu.VMEM(w.shape, w.dtype) for w in weights],
        in_specs=[ANY] * len(weights),
        out_specs=[VMEM] * len(weights),
        scratch_shapes=[pltpu.SemaphoreType.DMA((len(weights),))],
        compiler_params=pltpu.CompilerParams(vmem_limit_bytes=1 << 20),
        cost_estimate=pl.CostEstimate(
            flops=0, bytes_accessed=sum(2 * w.size for w in weights), transcendentals=0
        ),
        name="load",
    )(*[in_hbm(w) for w in weights])


def hidden_units(pieces, gate_w, up_w, rows_all, hidden, saved):
    put_together(pieces, rows_all)
    height = gate_w.shape[0]
    step = block_of(height)
    for j in range(height // step):
        part = pl.ds(j * step, step)
        gate = contract(gate_w[part], rows_all[...], 1, 1)
        up = contract(up_w[part], rows_all[...], 1, 1)
        if saved:
            saved[0][part] = gate
            saved[1][part] = up
        hidden[part] = (gate * jax.nn.sigmoid(gate) * up).astype(hidden.dtype)


def down_product(hidden, down_w, first, mine, theirs):
    half, wide = mine.shape
    tile = min(512, wide)
    across = hidden[...].T
    for start in range(0, wide, tile):
        value = contract(across, down_w[:, pl.ds(first + start, tile)], 1, 0)
        mine[:, start : start + tile] = value[:half]
        theirs[:, start : start + tile] = value[half:].astype(theirs.dtype)


def student_kernel(count, *refs):
    gate_w, up_w, down_hbm, down_w, rows_all, pre_gate, pre_up, hidden = refs[count : count + 8]
    mine, theirs, sem = refs[count + 8 :]
    fill = pltpu.make_async_copy(down_hbm, down_w, sem)
    fill.start()
    hidden_units(refs[:count], gate_w, up_w, rows_all, hidden, (pre_gate, pre_up))
    fill.wait()
    down_product(hidden, down_w, 0, mine, theirs)


def teacher_kernel(count, *refs):
    gate_w, up_w, hidden, rows_all = refs[count:]
    hidden_units(refs[:count], gate_w, up_w, rows_all, hidden, ())


def product_call(kernel, operands, in_specs, shapes, scratch, flops, grant):
    return pl.pallas_call(
        kernel,
        out_shape=shapes,
        in_specs=in_specs,
        out_specs=[VMEM] * len(shapes),
        scratch_shapes=scratch,
        compiler_params=pltpu.CompilerParams(vmem_limit_bytes=grant << 20),
        cost_estimate=pl.CostEstimate(
            flops=flops, bytes_accessed=flops // 128, transcendentals=0
        ),
    )(*operands)


def halves(rows, wide):
    return [
        jax.ShapeDtypeStruct((rows // 2, wide), jnp.float32),
        jax.ShapeDtypeStruct((rows // 2, wide), jnp.bfloat16),
    ]


def student_forward(pieces, gate_w, up_w, down_w):
    height, depth = gate_w.shape
    rows = len(pieces) * pieces[0].shape[0]
    shapes = [
        pltpu.VMEM((height, depth), jnp.bfloat16),
        jax.ShapeDtypeStruct((rows, depth), jnp.bfloat16),
        jax.ShapeDtypeStruct((height, rows), jnp.float32),
        jax.ShapeDtypeStruct((height, rows), jnp.float32),
        jax.ShapeDtypeStruct((height, rows), jnp.bfloat16),
    ] + halves(rows, depth)
    return product_call(
        functools.partial(student_kernel, len(pieces)),
        [*pieces, in_vmem(gate_w), in_vmem(up_w), in_hbm(down_w)],
        [VMEM] * (len(pieces) + 2) + [ANY],
        shapes,
        [pltpu.SemaphoreType.DMA],
        6 * rows * height * depth,
        12,
    )


def teacher_hidden(pieces, gate_w, up_w):
    height, depth = gate_w.shape
    rows = len(pieces) * pieces[0].shape[0]
    return product_call(
        functools.partial(teacher_kernel, len(pieces)),
        [*pieces, in_vmem(gate_w), in_vmem(up_w)],
        [VMEM] * (len(pieces) + 2),
        [jax.ShapeDtypeStruct((height, rows), jnp.bfloat16)],
        [pltpu.VMEM((rows, depth), jnp.bfloat16)],
        4 * rows * height * depth,
        12,
    )[0]


def teacher_down(hidden, down_w, first, wide):
    height, rows = hidden.shape
    return product_call(
        lambda hidden, down_w, *outs: down_product(hidden, down_w, first, *outs),
        [hidden, in_vmem(down_w)],
        [VMEM] * 2,
        halves(rows, wide),
        [],
        2 * rows * height * wide,
        8,
    )


def backward_kernel(count, first, final, start, *refs):
    pieces, refs = refs[:count], list(refs[count:])
    hidden, down_w = refs[:2]
    refs = refs[2:]
    if not first:
        before = refs[0]
        refs = refs[2:]
    if final:
        pre_gate, pre_up, rows_all = refs[:3]
        refs = refs[3:]
        grad_down, grad_gate, grad_up = refs[:3]
        refs = refs[3:]
        cotangent, stage_down, stage_gate, stage_up, sems = refs
    else:
        grad_down, after = refs[:2]
        cotangent, stage_down, sems = refs[2:]
    height = hidden.shape[0]
    wide = cotangent.shape[1]
    columns = pl.ds(start, wide)
    step = block_of(height)
    blocks = height // step
    put_together(pieces, cotangent)
    copies = []

    def send(source, target):
        copies.append(pltpu.make_async_copy(source, target, sems.at[len(copies)]))
        copies[-1].start()

    for j in range(blocks):
        part = pl.ds(j * step, step)
        stage_down[part] = contract(hidden[part], cotangent[...], 1, 0).astype(jnp.bfloat16)
        send(stage_down.at[part], grad_down.at[part, columns])
    for j in range(blocks):
        part = pl.ds(j * step, step)
        d_hidden = contract(down_w[part, columns], cotangent[...], 1, 1)
        if not first:
            d_hidden = d_hidden + before[part]
        if not final:
            after[part] = d_hidden
            continue
        gate, up = pre_gate[part], pre_up[part]
        sigma = jax.nn.sigmoid(gate)
        d_gate = (d_hidden * up * sigma * (1.0 + gate * (1.0 - sigma))).astype(jnp.bfloat16)
        d_up = (d_hidden * gate * sigma).astype(jnp.bfloat16)
        stage_gate[part] = contract(d_gate, rows_all[...], 1, 0).astype(jnp.bfloat16)
        send(stage_gate.at[part], grad_gate.at[part])
        stage_up[part] = contract(d_up, rows_all[...], 1, 0).astype(jnp.bfloat16)
        send(stage_up.at[part], grad_up.at[part])
    for copy in copies:
        copy.wait()


def backward(pieces, hidden, down_w, carried, saved, start):
    height, depth = down_w.shape
    rows = hidden.shape[1]
    wide = pieces[0].shape[1]
    blocks = height // block_of(height)
    first, final = carried is None, saved is not None
    operands = list(pieces) + [hidden, in_vmem(down_w)]
    in_specs = [VMEM] * (len(pieces) + 2)
    aliases = {}
    if not first:
        aliases = {len(operands) + 1: 0}
        operands += [carried[0], in_hbm(carried[1])]
        in_specs += [VMEM, ANY]
    whole = jax.ShapeDtypeStruct((height, depth), jnp.bfloat16)
    scratch = [
        pltpu.VMEM((rows, wide), jnp.bfloat16),
        pltpu.VMEM((height, wide), jnp.bfloat16),
    ]
    sends = blocks
    if final:
        operands += list(saved)
        in_specs += [VMEM] * 3
        shapes, out_specs = [whole] * 3, [ANY] * 3
        scratch += [pltpu.VMEM((height, depth), jnp.bfloat16)] * 2
        sends = 3 * blocks
    else:
        shapes = [whole, jax.ShapeDtypeStruct((height, rows), jnp.float32)]
        out_specs = [ANY, VMEM]
    scratch += [pltpu.SemaphoreType.DMA((sends,))]
    products = 4 * wide + (4 * depth if final else 0)
    return pl.pallas_call(
        functools.partial(backward_kernel, len(pieces), first, final, start),
        out_shape=shapes,
        in_specs=in_specs,
        out_specs=out_specs,
        scratch_shapes=scratch,
        input_output_aliases=aliases,
        compiler_params=pltpu.CompilerParams(vmem_limit_bytes=(26 if final else 8) << 20),
        cost_estimate=pl.CostEstimate(
            flops=products * rows * height,
            bytes_accessed=products * height,
            transcendentals=rows * height if final else 0,
        ),
    )(*operands)


def local(partner, tokens, w_gate, w_up, w_down):
    rows = tokens[0]
    gate_w, up_w, down_w = w_gate[0], w_up[0], w_down[0]
    replicas = lax.axis_size("replica")
    members = lax.axis_size("fsdp")
    chips = members // 2
    scale = 1.0 / math.sqrt(rows.shape[0] * members)
    foreign = small_call(
        foreign_kernel,
        spread(rows, replicas),
        jax.ShapeDtypeStruct(rows.shape, rows.dtype),
        partner,
    )
    gate_w, up_w = load(gate_w, up_w)
    own = with_other_core(gather_doubling(rows, chips), members)
    down_w, rows_all, pre_gate, pre_up, hidden, mine, theirs = student_forward(
        own, gate_w, up_w, down_w
    )
    student = scatter_halving(mine, theirs, chips, members)
    other = with_other_core(gather_direct(foreign, chips), members)
    teacher_units = teacher_hidden(other, gate_w, up_w)
    wide = rows.shape[1] // CHUNKS
    part = jax.ShapeDtypeStruct((rows.shape[0], wide), jnp.bfloat16)
    carried = None
    for c in range(CHUNKS):
        mine, theirs = teacher_down(teacher_units, down_w, c * wide, wide)
        terms = scatter_direct(mine, theirs, chips, members)
        taught = small_call(sum_kernel, terms, part)
        cotangent = small_call(
            functools.partial(cotangent_kernel, len(student), c * wide, scale),
            student + spread(taught, replicas),
            part,
            partner,
        )
        mine = gather_direct(cotangent, chips)
        pieces = with_other_core(mine, members)
        saved = (pre_gate, pre_up, rows_all) if c == CHUNKS - 1 else None
        grads = backward(pieces, hidden, down_w, carried, saved, c * wide)
        carried = (grads[1], grads[0])
    grad_down, grad_gate, grad_up = grads
    return (grad_gate[None], grad_up[None], grad_down[None])


def solution(mesh):
    in_specs = (P(),) + (P("replica", "fsdp", None),) * 4
    out_specs = (P("replica", "fsdp", None),) * 3
    return jax.shard_map(local, mesh=mesh, in_specs=in_specs, out_specs=out_specs, check_vma=False)
```

```python
import functools
import math

import jax
import jax.numpy as jnp
from jax import lax
from jax.experimental import pallas as pl
from jax.experimental.pallas import tpu as pltpu
from jax.sharding import PartitionSpec as P


SHARES = (3, 5)
CHUNKS = len(SHARES)
ANY = pl.BlockSpec(memory_space=pl.ANY)
VMEM = pl.BlockSpec(memory_space=pltpu.VMEM)


def exchange(value, axis, step, stride, count):
    pairs = [
        ((i ^ step) * stride + low, i * stride + low) for i in range(count) for low in range(stride)
    ]
    return lax.ppermute(value, axis, pairs)


def levels(count):
    assert count & (count - 1) == 0
    return [1 << level for level in range(count.bit_length() - 1)]


def arrangement(count):
    order = [0]
    for step in levels(count)[::-1]:
        order += [held + step for held in order]
    return order


def swap(value, members):
    return lax.ppermute(value, "fsdp", [(i, i ^ 1) for i in range(members)])


def gather_direct(rows, chips):
    mine = [rows]
    for step in arrangement(chips)[1:]:
        mine.append(exchange(rows, "fsdp", step, 2, chips))
    return mine


def gather_doubling(rows, chips):
    mine = [rows]
    for step in levels(chips)[::-1]:
        fresh = []
        for piece in mine:
            fresh.append(exchange(piece, "fsdp", step, 2, chips))
        mine += fresh
    return mine


def with_other_core(mine, members):
    theirs = []
    for piece in mine:
        theirs.append(swap(piece, members))
    return mine + theirs


def chip_sum(mine, theirs, chips, kept, members):
    other = swap(theirs, members)
    rows, wide = mine.shape[0] // chips, mine.shape[1]
    part = jax.ShapeDtypeStruct((rows, wide), jnp.bfloat16)
    return small_call(
        chip_kernel,
        [mine, other],
        [jax.ShapeDtypeStruct((rows, wide), jnp.float32)] * kept + [part] * (chips - kept),
    )


def scatter_direct(mine, theirs, chips, members):
    terms = list(chip_sum(mine, theirs, chips, 1, members))
    for i, step in enumerate(arrangement(chips)[1:]):
        terms[i + 1] = exchange(terms[i + 1], "fsdp", step, 2, chips)
    return terms


def scatter_halving(mine, theirs, chips, members):
    first = chip_sum(mine, theirs, chips, chips // 2, members)
    part = jax.ShapeDtypeStruct(first[0].shape, jnp.bfloat16)
    terms = [[term] for term in first]
    for step in levels(chips):
        kept = len(terms) // 2
        for i in reversed(range(kept)):
            sent = terms[kept + i]
            if len(sent) > 1:
                sent = [small_call(sum_kernel, sent, part)]
            terms[i].append(exchange(sent[0], "fsdp", step, 2, chips))
        terms = terms[:kept]
    return terms[0]


def spread(value, replicas):
    others = []
    for step in range(1, replicas):
        others.append(exchange(value, "replica", step, 1, replicas))
    return others


def small_call(kernel, operands, shapes, partner=None):
    head = [] if partner is None else [partner]
    flat = shapes if isinstance(shapes, list) else [shapes]
    size = sum(x.size for x in operands) + sum(x.size for x in flat)
    return pl.pallas_call(
        kernel,
        out_shape=shapes,
        in_specs=[pl.BlockSpec(memory_space=pltpu.SMEM)] * len(head) + [VMEM] * len(operands),
        out_specs=[VMEM] * len(flat) if isinstance(shapes, list) else VMEM,
        compiler_params=pltpu.CompilerParams(vmem_limit_bytes=4 << 20),
        cost_estimate=pl.CostEstimate(flops=size, bytes_accessed=2 * size, transcendentals=0),
    )(*head, *operands)


def chip_kernel(mine, other, own, *pieces):
    rows = own.shape[0]
    for k, target in enumerate((own,) + pieces):
        part = pl.ds(k * rows, rows)
        target[...] = (mine[part] + other[part].astype(jnp.float32)).astype(target.dtype)


def sum_kernel(*refs):
    total = refs[0][...]
    for term in refs[1:-1]:
        total = total + term[...].astype(jnp.float32)
    refs[-1][...] = total.astype(refs[-1].dtype)


def choose(candidates, masks):
    chosen = candidates[0][...]
    for k in range(1, len(candidates)):
        mask = jnp.tile(masks[k], (1, chosen.shape[1] // masks.shape[2]))
        chosen = jnp.where(mask > 0, candidates[k][...], chosen)
    return chosen


def foreign_kernel(partner, *refs):
    replicas = partner.shape[0]
    here = lax.axis_index("replica")
    taught = sum(jnp.where(partner[r] == here, r, 0) for r in range(replicas))
    taught_by = sum(jnp.where(here == r, partner[r], 0) for r in range(replicas))
    candidates, target, masks = refs[:-2], refs[-2], refs[-1]
    chosen = candidates[0][...]
    for k in range(1, len(candidates)):
        chosen = jnp.where((here ^ taught) == k + 1, candidates[k][...], chosen)
    target[...] = chosen
    for k in range(replicas - 1):
        hit = jnp.where((here ^ taught_by) == k + 1, 1, 0)
        masks[k] = jnp.full(masks.shape[1:], hit, masks.dtype)


def cotangent_kernel(count, start, scale, masks, *refs):
    target = refs[-1]
    columns = pl.ds(start, target.shape[1])
    student = refs[0][:, columns]
    for term in refs[1:count]:
        student = student + term[:, columns].astype(jnp.float32)
    teacher = choose(refs[count:-1], masks).astype(jnp.float32)
    target[...] = ((student - teacher) * scale).astype(target.dtype)


def contract(left, right, left_dim, right_dim):
    return lax.dot_general(
        left, right, (((left_dim,), (right_dim,)), ((), ())), preferred_element_type=jnp.float32
    )


def block_of(count):
    return 128 if count % 128 == 0 else count


def put_together(pieces, whole):
    rows = pieces[0].shape[0]
    for i, piece in enumerate(pieces):
        whole[i * rows : (i + 1) * rows, :] = piece[...]


def load_kernel(*refs):
    count = len(refs) // 2
    sems = refs[-1]
    copies = [
        pltpu.make_async_copy(refs[i], refs[count + i], sems.at[i]) for i in range(count)
    ]
    for copy in copies:
        copy.start()
    for copy in copies:
        copy.wait()


def in_hbm(array):
    return pltpu.with_memory_space_constraint(array, pltpu.HBM)


def in_vmem(array):
    return pltpu.with_memory_space_constraint(array, pltpu.VMEM)


def load(*weights):
    return pl.pallas_call(
        load_kernel,
        out_shape=[pltpu.VMEM(w.shape, w.dtype) for w in weights],
        in_specs=[ANY] * len(weights),
        out_specs=[VMEM] * len(weights),
        scratch_shapes=[pltpu.SemaphoreType.DMA((len(weights),))],
        compiler_params=pltpu.CompilerParams(vmem_limit_bytes=1 << 20),
        cost_estimate=pl.CostEstimate(
            flops=0, bytes_accessed=sum(2 * w.size for w in weights), transcendentals=0
        ),
        name="load",
    )(*[in_hbm(w) for w in weights])


def hidden_units(pieces, gate_w, up_w, rows_all, hidden, saved):
    put_together(pieces, rows_all)
    height = gate_w.shape[0]
    step = block_of(height)
    for j in range(height // step):
        part = pl.ds(j * step, step)
        gate = contract(gate_w[part], rows_all[...], 1, 1)
        up = contract(up_w[part], rows_all[...], 1, 1)
        if saved:
            saved[0][part] = gate
            saved[1][part] = up
        hidden[part] = (gate * jax.nn.sigmoid(gate) * up).astype(hidden.dtype)


def down_product(hidden, down_w, first, mine, theirs):
    half, wide = mine.shape
    tile = math.gcd(512, wide)
    across = hidden[...].T
    for start in range(0, wide, tile):
        value = contract(across, down_w[:, pl.ds(first + start, tile)], 1, 0)
        mine[:, start : start + tile] = value[:half]
        theirs[:, start : start + tile] = value[half:].astype(theirs.dtype)


def student_kernel(count, *refs):
    gate_w, up_w, down_hbm, down_w, rows_all, pre_gate, pre_up, hidden = refs[count : count + 8]
    mine, theirs, sem = refs[count + 8 :]
    fill = pltpu.make_async_copy(down_hbm, down_w, sem)
    fill.start()
    hidden_units(refs[:count], gate_w, up_w, rows_all, hidden, (pre_gate, pre_up))
    fill.wait()
    down_product(hidden, down_w, 0, mine, theirs)


def teacher_kernel(count, *refs):
    gate_w, up_w, hidden, rows_all = refs[count:]
    hidden_units(refs[:count], gate_w, up_w, rows_all, hidden, ())


def product_call(kernel, operands, in_specs, shapes, scratch, flops, grant):
    return pl.pallas_call(
        kernel,
        out_shape=shapes,
        in_specs=in_specs,
        out_specs=[VMEM] * len(shapes),
        scratch_shapes=scratch,
        compiler_params=pltpu.CompilerParams(vmem_limit_bytes=grant << 20),
        cost_estimate=pl.CostEstimate(
            flops=flops, bytes_accessed=flops // 128, transcendentals=0
        ),
    )(*operands)


def halves(rows, wide):
    return [
        jax.ShapeDtypeStruct((rows // 2, wide), jnp.float32),
        jax.ShapeDtypeStruct((rows // 2, wide), jnp.bfloat16),
    ]


def student_forward(pieces, gate_w, up_w, down_w):
    height, depth = gate_w.shape
    rows = len(pieces) * pieces[0].shape[0]
    shapes = [
        pltpu.VMEM((height, depth), jnp.bfloat16),
        jax.ShapeDtypeStruct((rows, depth), jnp.bfloat16),
        jax.ShapeDtypeStruct((height, rows), jnp.float32),
        jax.ShapeDtypeStruct((height, rows), jnp.float32),
        jax.ShapeDtypeStruct((height, rows), jnp.bfloat16),
    ] + halves(rows, depth)
    return product_call(
        functools.partial(student_kernel, len(pieces)),
        [*pieces, in_vmem(gate_w), in_vmem(up_w), in_hbm(down_w)],
        [VMEM] * (len(pieces) + 2) + [ANY],
        shapes,
        [pltpu.SemaphoreType.DMA],
        6 * rows * height * depth,
        12,
    )


def teacher_hidden(pieces, gate_w, up_w):
    height, depth = gate_w.shape
    rows = len(pieces) * pieces[0].shape[0]
    return product_call(
        functools.partial(teacher_kernel, len(pieces)),
        [*pieces, in_vmem(gate_w), in_vmem(up_w)],
        [VMEM] * (len(pieces) + 2),
        [jax.ShapeDtypeStruct((height, rows), jnp.bfloat16)],
        [pltpu.VMEM((rows, depth), jnp.bfloat16)],
        4 * rows * height * depth,
        12,
    )[0]


def teacher_down(hidden, down_w, first, wide):
    height, rows = hidden.shape
    return product_call(
        lambda hidden, down_w, *outs: down_product(hidden, down_w, first, *outs),
        [hidden, in_vmem(down_w)],
        [VMEM] * 2,
        halves(rows, wide),
        [],
        2 * rows * height * wide,
        8,
    )


def backward_kernel(count, first, final, start, *refs):
    pieces, refs = refs[:count], list(refs[count:])
    hidden, down_w = refs[:2]
    refs = refs[2:]
    if not first:
        before = refs[0]
        refs = refs[2:]
    if final:
        pre_gate, pre_up, rows_all = refs[:3]
        refs = refs[3:]
        grad_down, grad_gate, grad_up = refs[:3]
        refs = refs[3:]
        cotangent, stage_down, stage_gate, stage_up, sems = refs
    else:
        grad_down, after = refs[:2]
        cotangent, stage_down, sems = refs[2:]
    height = hidden.shape[0]
    wide = cotangent.shape[1]
    columns = pl.ds(start, wide)
    step = block_of(height)
    blocks = height // step
    put_together(pieces, cotangent)
    copies = []

    def send(source, target):
        copies.append(pltpu.make_async_copy(source, target, sems.at[len(copies)]))
        copies[-1].start()

    for j in range(blocks):
        part = pl.ds(j * step, step)
        stage_down[part] = contract(hidden[part], cotangent[...], 1, 0).astype(jnp.bfloat16)
        send(stage_down.at[part], grad_down.at[part, columns])
    for j in range(blocks):
        part = pl.ds(j * step, step)
        d_hidden = contract(down_w[part, columns], cotangent[...], 1, 1)
        if not first:
            d_hidden = d_hidden + before[part]
        if not final:
            after[part] = d_hidden
            continue
        gate, up = pre_gate[part], pre_up[part]
        sigma = jax.nn.sigmoid(gate)
        d_gate = (d_hidden * up * sigma * (1.0 + gate * (1.0 - sigma))).astype(jnp.bfloat16)
        d_up = (d_hidden * gate * sigma).astype(jnp.bfloat16)
        stage_gate[part] = contract(d_gate, rows_all[...], 1, 0).astype(jnp.bfloat16)
        send(stage_gate.at[part], grad_gate.at[part])
        stage_up[part] = contract(d_up, rows_all[...], 1, 0).astype(jnp.bfloat16)
        send(stage_up.at[part], grad_up.at[part])
    for copy in copies:
        copy.wait()


def backward(pieces, hidden, down_w, carried, saved, start):
    height, depth = down_w.shape
    rows = hidden.shape[1]
    wide = pieces[0].shape[1]
    blocks = height // block_of(height)
    first, final = carried is None, saved is not None
    operands = list(pieces) + [hidden, in_vmem(down_w)]
    in_specs = [VMEM] * (len(pieces) + 2)
    aliases = {}
    if not first:
        aliases = {len(operands) + 1: 0}
        operands += [carried[0], in_hbm(carried[1])]
        in_specs += [VMEM, ANY]
    whole = jax.ShapeDtypeStruct((height, depth), jnp.bfloat16)
    scratch = [
        pltpu.VMEM((rows, wide), jnp.bfloat16),
        pltpu.VMEM((height, wide), jnp.bfloat16),
    ]
    sends = blocks
    if final:
        operands += list(saved)
        in_specs += [VMEM] * 3
        shapes, out_specs = [whole] * 3, [ANY] * 3
        scratch += [pltpu.VMEM((height, depth), jnp.bfloat16)] * 2
        sends = 3 * blocks
    else:
        shapes = [whole, jax.ShapeDtypeStruct((height, rows), jnp.float32)]
        out_specs = [ANY, VMEM]
    scratch += [pltpu.SemaphoreType.DMA((sends,))]
    products = 4 * wide + (4 * depth if final else 0)
    return pl.pallas_call(
        functools.partial(backward_kernel, len(pieces), first, final, start),
        out_shape=shapes,
        in_specs=in_specs,
        out_specs=out_specs,
        scratch_shapes=scratch,
        input_output_aliases=aliases,
        compiler_params=pltpu.CompilerParams(vmem_limit_bytes=(26 if final else 8) << 20),
        cost_estimate=pl.CostEstimate(
            flops=products * rows * height,
            bytes_accessed=products * height,
            transcendentals=rows * height if final else 0,
        ),
    )(*operands)


def local(partner, tokens, w_gate, w_up, w_down):
    rows = tokens[0]
    gate_w, up_w, down_w = w_gate[0], w_up[0], w_down[0]
    replicas = lax.axis_size("replica")
    members = lax.axis_size("fsdp")
    chips = members // 2
    scale = 1.0 / math.sqrt(rows.shape[0] * members)
    foreign, taught_by = small_call(
        foreign_kernel,
        spread(rows, replicas),
        [
            jax.ShapeDtypeStruct(rows.shape, rows.dtype),
            jax.ShapeDtypeStruct((replicas - 1, rows.shape[0], 128), jnp.int32),
        ],
        partner,
    )
    gate_w, up_w = load(gate_w, up_w)
    own = with_other_core(gather_doubling(rows, chips), members)
    down_w, rows_all, pre_gate, pre_up, hidden, mine, theirs = student_forward(
        own, gate_w, up_w, down_w
    )
    student = scatter_halving(mine, theirs, chips, members)
    other = with_other_core(gather_direct(foreign, chips), members)
    teacher_units = teacher_hidden(other, gate_w, up_w)
    carried, start = None, 0
    for c in range(CHUNKS):
        wide = rows.shape[1] * SHARES[c] // sum(SHARES)
        part = jax.ShapeDtypeStruct((rows.shape[0], wide), jnp.bfloat16)
        mine, theirs = teacher_down(teacher_units, down_w, start, wide)
        terms = scatter_direct(mine, theirs, chips, members)
        taught_sum = small_call(sum_kernel, terms, part)
        cotangent = small_call(
            functools.partial(cotangent_kernel, len(student), start, scale),
            [taught_by] + student + spread(taught_sum, replicas),
            part,
        )
        mine = gather_direct(cotangent, chips)
        pieces = with_other_core(mine, members)
        saved = (pre_gate, pre_up, rows_all) if c == CHUNKS - 1 else None
        grads = backward(pieces, hidden, down_w, carried, saved, start)
        carried, start = (grads[1], grads[0]), start + wide
    grad_down, grad_gate, grad_up = grads
    return (grad_gate[None], grad_up[None], grad_down[None])


def solution(mesh):
    in_specs = (P(),) + (P("replica", "fsdp", None),) * 4
    out_specs = (P("replica", "fsdp", None),) * 3
    return jax.shard_map(local, mesh=mesh, in_specs=in_specs, out_specs=out_specs, check_vma=False)
```
